128 devices in a mesh: ctx: 8 (over x, core), tp: 16 (over y, z).
Axes of the slice: x: 4, y: 4, z: 4, core: 2. Of those that a mesh axis runs over, the one named last changes fastest.
Arguments:
- streams: bfloat16 [3, 8192, 8192], P(None, 'ctx', 'tp'), may hold values from -6 to 6
- conv_weight: float32 [3, 3, 8192], P(None, None, 'tp'), may hold values from -3.5 to 3.5
- skip_weight: float32 [8192], P('tp'), may hold values from -4 to 4
- long_filter: bfloat16 [8192, 8192], P('ctx', 'tp'), may hold values from -1.6 to 1.6
- out_weight: bfloat16 [8192, 8192], P('tp'), may hold values from -0.09375 to 0.09375
Outputs:
- projected: bfloat16 [8192, 8192], P('ctx', 'tp')
The draws below stay inside these ranges and needn't reach their ends.
All inputs are finite; a program needn't handle non-finite values.
Results may differ from the reference program's by a relative error of at most 0.015.
Values may be sent and summed in bfloat16 or wider, within the bound.
A program may use at most 128 MiB of HBM per device.

```python
import jax
import jax.numpy as jnp
from jax import lax

D = 8192
KCONV = 3
SEQUENCE_LENGTH = 8192


def draw_long_filter(key, part):
    gradual_decay_key, decay_rate_key, quick_decay_key, spike_key, jitter_key = jax.random.split(jax.random.fold_in(key, 7101), 5)
    slow_share = 0.5
    slow_pick = jax.random.bernoulli(gradual_decay_key, slow_share, (D,))
    slow_rate = jnp.exp(jax.random.uniform(decay_rate_key, (D,), jnp.float32, jnp.log(0.25 / SEQUENCE_LENGTH), jnp.log(2.0 / SEQUENCE_LENGTH)))
    fast_rate = jnp.exp(jax.random.uniform(quick_decay_key, (D,), jnp.float32, jnp.log(1.0 / 50.0), jnp.log(1.0 / 20.0)))
    decay_rates = jnp.where(slow_pick, slow_rate, fast_rate)
    spike_events = jax.random.randint(spike_key, (3,), 1, SEQUENCE_LENGTH)
    offset_steps = jnp.arange(SEQUENCE_LENGTH, dtype=jnp.int32)
    returned_filter = (offset_steps[:, None] >= spike_events[None, :]).astype(jnp.float32)
    spike_multiplier = jnp.exp(jnp.log(0.6) * (returned_filter[:, 0] + returned_filter[:, 1] + returned_filter[:, 2]))
    decay_profile = jnp.exp(-decay_rates[None, :] * offset_steps.astype(jnp.float32)[:, None]) * spike_multiplier[:, None]
    scale_sq = (1.0 - jnp.exp(-2.0 * decay_rates * SEQUENCE_LENGTH)) / (1.0 - jnp.exp(-2.0 * decay_rates))
    noise = jnp.clip(jax.random.normal(jitter_key, (SEQUENCE_LENGTH, D), jnp.float32), -5.0, 5.0)
    return (noise * decay_profile / jnp.sqrt(scale_sq)[None, :]).astype(jnp.bfloat16)


def with_spikes(array, own_key, source, target, blocks, factor):
    owner, partner = [(jnp.arange(array.shape[position]) // (array.shape[position] // blocks)).reshape([-1 if axis == position else 1 for axis in range(array.ndim)]) for position in (source, target)]
    chosen = jax.random.permutation(own_key, blocks)[partner]
    strong = (owner == chosen) | (owner == (partner + blocks // 2) % blocks)
    return jnp.where(strong, factor * array, array)


def block_levels(key, dims, cuts, least, top_value):
    level, own = 1.0, jax.random.fold_in(key, 6)
    for position, parts in cuts:
        draws = jnp.exp(jax.random.uniform(jax.random.fold_in(own, position), (parts,), jnp.float32, least / len(cuts), top_value / len(cuts)))
        level = level * jnp.repeat(draws, dims[position] // parts).reshape([-1 if axis == position else 1 for axis in range(len(dims))])
    return level


def centred(rng, extent, width, reach, cuts=(), kind=jnp.bfloat16):
    entries = jax.random.normal(rng, extent, jnp.float32) * width
    if len(cuts) > 0:
        entries = block_levels(rng, extent, cuts, -0.22, 0.18) * entries
    return jnp.clip(entries, min=-reach, max=reach).astype(kind)


def bell_draw_with(rng, dims, scale, limit, cuts, heavy, kind=jnp.bfloat16):
    drawn = scale * jax.random.normal(rng, dims, jnp.float32)
    if cuts:
        drawn = drawn * block_levels(rng, dims, cuts, -0.22, 0.18)
    return jnp.clip(with_spikes(drawn, jax.random.fold_in(rng, 3), *heavy), -limit, limit).astype(kind)


def setup_inputs(seed: int = 0) -> dict:
    splits = jax.random.split(jax.random.key(seed), 6)
    streams = centred(splits[0], (3, SEQUENCE_LENGTH, D), 1.0, 6.0, ((1, 8), (2, 16)))
    conv_weight = centred(splits[1], (3, KCONV, D), KCONV ** -0.5, 3.5, ((2, 16),), jnp.float32)
    skip_weight = centred(splits[2], (D,), 1.0, 4.0, ((0, 16),), jnp.float32)
    long_filter = draw_long_filter(jax.random.fold_in(splits[5], 71), 0)
    out_weight = bell_draw_with(splits[4], (D, D), D ** -0.5, 0.09375, ((0, 16),), (0, 1, 16, 2.0))
    return dict(streams=streams, conv_weight=conv_weight, skip_weight=skip_weight, long_filter=long_filter, out_weight=out_weight)


def short_conv(streams, conv_weight):
    values = streams.astype(jnp.float32)
    padded = jnp.pad(values, ((0, 0), (KCONV - 1, 0), (0, 0)))
    summed = jnp.zeros(values.shape, jnp.float32)
    for lag_step in range(KCONV):
        begin = KCONV - 1 - lag_step
        summed = summed + conv_weight[:, lag_step, None, :].astype(jnp.float32) * padded[:, begin:begin + SEQUENCE_LENGTH, :]
    return summed


def long_conv(mixed_u, long_filter):
    block_width = min(D, 512)
    block_count = D // block_width
    signal = mixed_u.astype(jnp.float32).reshape(SEQUENCE_LENGTH, block_count, block_width).transpose(1, 0, 2)
    kernel = long_filter.astype(jnp.float32).reshape(SEQUENCE_LENGTH, block_count, block_width).transpose(1, 0, 2)

    def one_block(pair):
        sig_block, ker_block = pair
        spec_sig = jnp.fft.rfft(sig_block, n=2 * SEQUENCE_LENGTH, axis=0)
        spec_ker = jnp.fft.rfft(ker_block, n=2 * SEQUENCE_LENGTH, axis=0)
        return jnp.fft.irfft(spec_sig * spec_ker, n=2 * SEQUENCE_LENGTH, axis=0)[:SEQUENCE_LENGTH]

    result = lax.map(one_block, (signal, kernel))
    return result.transpose(1, 0, 2).reshape(SEQUENCE_LENGTH, D)


def reference(streams, conv_weight, skip_weight, long_filter, out_weight):
    conv_out = short_conv(streams, conv_weight)
    gating = conv_out[0]
    mixed_u = (conv_out[1] * conv_out[2]).astype(jnp.bfloat16)
    long_out = long_conv(mixed_u, long_filter).astype(jnp.bfloat16)
    gated = ((long_out.astype(jnp.float32) + skip_weight[None, :] * mixed_u.astype(jnp.float32)) * gating).astype(jnp.bfloat16)
    return jnp.dot(gated, out_weight, preferred_element_type=jnp.float32).astype(jnp.bfloat16)
```

```python
import functools
import math

import jax
import jax.numpy as jnp
import ml_dtypes
import numpy as np
from jax import lax
from jax.experimental import pallas as pl
from jax.experimental.pallas import tpu as pltpu
from jax.sharding import PartitionSpec as P

BF = jnp.bfloat16
F32 = jnp.float32
MESH = pl.DeviceIdType.MESH

ROWS = 1024
CH = 512
CTX = 8
NY = 4
NZ = 4
LC = CH // CTX
TILES = ROWS // 128
NA = 64
GROUPS = LC // 4
NC = 8
CR = ROWS // NC


def tables():
    k1 = np.arange(64) + 0.25
    a = np.arange(64)
    b = np.arange(128)
    th1 = 2 * np.pi * np.outer(k1, a) / 64
    c1, s1 = np.cos(th1), np.sin(th1)
    eye = np.eye(4)
    f1 = np.concatenate([np.kron(eye, c1), np.kron(eye, s1)], axis=0)
    th2 = 2 * np.pi * np.outer(b, b) / 128
    c2, s2 = np.cos(th2), np.sin(th2)
    f2 = np.block([[c2, s2], [-s2, c2]])
    f2i = np.block([[c2, -s2], [s2, c2]])
    inv = np.concatenate([np.kron(eye, c1.T), np.kron(eye, s1.T)], axis=1) / 8192.0
    inv = inv.reshape(4, 8, 8, 512).transpose(1, 0, 2, 3).reshape(256, 512)
    tw = 2 * np.pi * np.outer(k1, b) / 8192
    twc, tws = np.tile(np.cos(tw), (4, 1)), np.tile(np.sin(tw), (4, 1))
    bf = lambda m: jnp.asarray(m.astype(np.float32).astype(ml_dtypes.bfloat16))
    return (
        bf(f1),
        bf(f2),
        bf(f2i),
        bf(inv),
        jnp.asarray(twc.astype(np.float32)),
        jnp.asarray(tws.astype(np.float32)),
        bf(np.eye(256)),
    )


def nt(a, b):
    return lax.dot_general(a, b, (((1,), (1,)), ((), ())), preferred_element_type=F32)


def mm(a, b):
    return jnp.dot(a, b, preferred_element_type=F32)


def kernel(
    x_ref, h_ref, cw_ref, skip_ref, w_ref, f1_ref, f2_ref, f2i_ref, f1i_ref, twc_ref, tws_ref, eye_ref,
    out_ref,
    halo, x32, gat, upos, sh, su, rh, ru, r32, spec, ys, ry, wr, gall, sopp, ra, rb, sl, sr, rl, rr, part,
    halo_sem, h_ss, h_rs, h_ls, u_ss, u_rs, u_ls, y_ss, y_rs, y_ls,
    w_ss, w_rs, w_ls, f_ss, f_rs, ag_ss, ag_rs, fw_ss, fw_rs, r1_ss, r1_rs, r2_ss, r2_rs,
):
    me = lax.axis_index("ctx")
    tp = lax.axis_index("tp")
    y = tp // NZ
    z = tp % NZ
    core = me % 2
    sib = me + 1 - 2 * core

    def dev(ctx, yy, zz):
        return (ctx, yy * NZ + zz)

    def remote(src, dst, ss, rs, to):
        return pltpu.make_async_remote_copy(
            src_ref=src, dst_ref=dst, send_sem=ss, recv_sem=rs, device_id=to, device_id_type=MESH
        )

    barrier = pltpu.get_barrier_semaphore()
    for d in range(1, CTX):
        pl.semaphore_signal(barrier, inc=1, device_id=dev((me + d) % CTX, y, z), device_id_type=MESH)
    for d in range(1, NZ):
        pl.semaphore_signal(barrier, inc=1, device_id=dev(me, y, (z + d) % NZ), device_id_type=MESH)
    for d in (1, 3):
        pl.semaphore_signal(barrier, inc=1, device_id=dev(me, (y + d) % NY, z), device_id_type=MESH)
    pl.semaphore_wait(barrier, 12)

    halo_cp = remote(
        x_ref.at[:, ROWS - 16 :, :], halo, halo_sem.at[0], halo_sem.at[1], dev((me + 1) % CTX, y, z)
    )
    halo_cp.start()

    half = pl.multiple_of(core * (CH // 2), CH // 2)
    w_cps = []
    for d in range(1, NZ):
        zp = (z + d) % NZ
        for yb in range(NY):
            cols = pl.multiple_of((NZ * yb + zp) * CH, CH)
            w_cps.append(
                remote(
                    w_ref.at[pl.ds(half, CH // 2), pl.ds(cols, CH)],
                    wr.at[yb, pl.ds(z * CH + half, CH // 2), :],
                    w_ss.at[d - 1, yb],
                    w_rs.at[d - 1, yb],
                    dev(me, y, zp),
                )
            )
    for cp in w_cps:
        cp.start()
    w_local = []
    for yb in range(NY):
        cols = pl.multiple_of((NZ * yb + z) * CH, CH)
        w_local.append(
            pltpu.make_async_copy(w_ref.at[:, pl.ds(cols, CH)], wr.at[yb, pl.ds(z * CH, CH), :], w_ls.at[yb])
        )
    for cp in w_local:
        cp.start()

    def exchange(send, recv, ss, rs, ls):
        cps = []
        for d in (4, 3, 5, 2, 6, 1, 7):
            j = (me + d) % CTX
            cps.append(
                remote(
                    send.at[:, pl.ds(pl.multiple_of(j * LC, LC), LC), :],
                    recv.at[pl.ds(me * TILES, TILES)],
                    ss.at[d - 1],
                    rs.at[d - 1],
                    dev(j, y, z),
                )
            )
        own = pltpu.make_async_copy(
            send.at[:, pl.ds(pl.multiple_of(me * LC, LC), LC), :], recv.at[pl.ds(me * TILES, TILES)], ls.at[0]
        )
        return cps, own

    eye = eye_ref[...]
    for t in range(TILES):
        for q in range(CH // 256):
            sh[t, 256 * q : 256 * q + 256, :] = nt(
                eye, h_ref[128 * t : 128 * t + 128, 256 * q : 256 * q + 256]
            ).astype(BF)
    h_cps, h_own = exchange(sh, rh, h_ss, h_rs, h_ls)
    for cp in h_cps:
        cp.start()
    h_own.start()

    for s in (1, 2, 0):
        x32[s, 8:, :] = x_ref[s].astype(F32)
    halo_cp.wait()
    edge = halo[...].astype(F32)[:, 8:16, :]
    x32[:, 0:8, :] = jnp.where(me == 0, jnp.zeros_like(edge), edge)

    def short(s, t, q):
        cs = slice(256 * q, 256 * q + 256)
        base = 8 + 128 * t
        acc = cw_ref[s, 0:1, cs] * x32[s, base : base + 128, cs]
        acc = acc + cw_ref[s, 1:2, cs] * x32[s, base - 1 : base + 127, cs]
        return acc + cw_ref[s, 2:3, cs] * x32[s, base - 2 : base + 126, cs]

    for t in range(TILES):
        for q in range(CH // 256):
            u = (short(1, t, q) * short(2, t, q)).astype(BF)
            upos[128 * t : 128 * t + 128, 256 * q : 256 * q + 256] = u
            su[t, 256 * q : 256 * q + 256, :] = nt(eye, u).astype(BF)
    u_cps, u_own = exchange(su, ru, u_ss, u_rs, u_ls)
    for cp in u_cps:
        cp.start()
    u_own.start()

    for t in range(TILES):
        for q in range(CH // 256):
            gat[128 * t : 128 * t + 128, 256 * q : 256 * q + 256] = short(0, t, q)

    def load_group(g):
        rows = [r32[pl.ds(4 * g + i, NA, stride=LC), :] for i in range(4)]
        return jnp.concatenate(rows, axis=0).astype(BF)

    def forward(v):
        o = mm(f1_ref[...], v)
        re, im = o[:256], o[256:]
        c, s = twc_ref[...], tws_ref[...]
        lhs = jnp.concatenate([(re * c - im * s).astype(BF), (re * s + im * c).astype(BF)], axis=1)
        return mm(lhs, f2_ref[...])

    for cp in h_cps:
        cp.wait()
    h_own.wait()
    r32[...] = rh[...].astype(F32).reshape(NA * LC, 128)

    def filter_group(g, carry):
        spec[g] = forward(load_group(g))
        return carry

    lax.fori_loop(0, GROUPS, filter_group, 0)

    for cp in u_cps:
        cp.wait()
    u_own.wait()
    r32[...] = ru[...].astype(F32).reshape(NA * LC, 128)

    def signal_group(g):
        o = forward(load_group(g))
        f = spec[g]
        ur, ui = o[:, :128], o[:, 128:]
        hr, hi = f[:, :128], f[:, 128:]
        lhs = jnp.concatenate([(ur * hr - ui * hi).astype(BF), (ur * hi + ui * hr).astype(BF)], axis=1)
        v = mm(lhs, f2i_ref[...])
        vr, vi = v[:, :128], v[:, 128:]
        c, s = twc_ref[...], tws_ref[...]
        return jnp.concatenate([(vr * c + vi * s).astype(BF), (vi * c - vr * s).astype(BF)], axis=0)

    def signal_pair(i, carry):
        v = jnp.concatenate([signal_group(2 * i), signal_group(2 * i + 1)], axis=1)
        o = mm(f1i_ref[...], v).astype(BF)
        for k in range(2):
            ys[:, pl.ds(pl.multiple_of(64 * i + 32 * k, 32), 32), :] = o[:, 128 * k : 128 * k + 128].reshape(8, 32, 128)
        return carry

    lax.fori_loop(0, GROUPS // 2, signal_pair, 0)

    y_cps = []
    for d in (4, 3, 5, 2, 6, 1, 7):
        j = (me + d) % CTX
        y_cps.append(remote(ys.at[j], ry.at[me], y_ss.at[d - 1], y_rs.at[d - 1], dev(j, y, z)))
    for cp in y_cps:
        cp.start()
    y_own = pltpu.make_async_copy(ys.at[me], ry.at[me], y_ls.at[0])
    y_own.start()

    f_cps = []
    for d in range(1, NZ):
        zs = (z + NZ - d) % NZ
        for yb in range(NY):
            w_cps[(d - 1) * NY + yb].wait()
            blk = wr.at[yb, pl.ds(zs * CH + half, CH // 2), :]
            cp = remote(blk, blk, f_ss.at[d - 1, yb], f_rs.at[d - 1, yb], dev(sib, y, z))
            cp.start()
            f_cps.append(cp)

    for cp in y_cps:
        cp.wait()
    y_own.wait()
    r32[...] = ry[...].astype(F32).reshape(CTX * 512, 128)
    eye128 = eye_ref[0:128, 0:128]
    for t in range(TILES):
        long_out = nt(eye128, r32[pl.ds(t, CH, stride=8), :].astype(BF))
        rows = slice(128 * t, 128 * t + 128)
        gated = (long_out + skip_ref[...] * upos[rows, :].astype(F32)) * gat[rows, :]
        gall[z, rows, :] = gated.astype(BF)

    for cp in w_local:
        cp.wait()
    for cp in f_cps:
        cp.wait()

    zl, zr, zo = (z + 3) % NZ, (z + 1) % NZ, (z + 2) % NZ
    yl, yr, yo = (y + 3) % NY, (y + 1) % NY, (y + 2) % NY
    hr_ = CR // 2
    ag, fw, r1, r2 = {}, {}, {}, {}
    for i in range(NC + 4):
        if i < NC:
            blk = gall.at[z, i * CR : (i + 1) * CR, :]
            ag[i] = (
                remote(blk, blk, ag_ss.at[0, i], ag_rs.at[0, i], dev(me, y, zr)),
                remote(blk, blk, ag_ss.at[1, i], ag_rs.at[1, i], dev(me, y, zl)),
            )
            for cp in ag[i]:
                cp.start()
        c = i - 1
        if 0 <= c < NC:
            up = gall.at[zl, c * CR : c * CR + hr_, :]
            dn = gall.at[zr, c * CR + hr_ : (c + 1) * CR, :]
            fw[c] = (
                remote(up, up, fw_ss.at[0, c], fw_rs.at[0, c], dev(me, y, zr)),
                remote(dn, dn, fw_ss.at[1, c], fw_rs.at[1, c], dev(me, y, zl)),
            )
            for k in range(2):
                ag[c][k].wait_recv()
                fw[c][k].start()
        c = i - 2
        if 0 <= c < NC:
            for k in range(2):
                fw[c][k].wait_recv()

            def product(yb):
                acc = mm(gall[0, c * CR : (c + 1) * CR, :], wr[yb, 0:CH, :])
                for k in range(1, NZ):
                    acc = acc + mm(gall[k, c * CR : (c + 1) * CR, :], wr[yb, k * CH : (k + 1) * CH, :])
                return acc

            sopp[c] = product(yo).astype(BF)
            r1[c] = (
                remote(sopp.at[c, 0:hr_, :], ra.at[c], r1_ss.at[0, c], r1_rs.at[0, c], dev(me, yr, z)),
                remote(sopp.at[c, hr_:CR, :], rb.at[c], r1_ss.at[1, c], r1_rs.at[1, c], dev(me, yl, z)),
            )
            for cp in r1[c]:
                cp.start()
            part[c % 3, 1] = product(yr)
            part[c % 3, 2] = product(yl)
            part[c % 3, 0] = product(y)
        c = i - 3
        if 0 <= c < NC:
            p = c % 3
            r1[c][0].wait_recv()
            sr[c, 0:hr_, :] = (part[p, 1, 0:hr_, :] + ra[c].astype(F32)).astype(BF)
            sr[c, hr_:CR, :] = part[p, 1, hr_:CR, :].astype(BF)
            r1[c][1].wait_recv()
            sl[c, hr_:CR, :] = (part[p, 2, hr_:CR, :] + rb[c].astype(F32)).astype(BF)
            sl[c, 0:hr_, :] = part[p, 2, 0:hr_, :].astype(BF)
            r2[c] = (
                remote(sr.at[c], rl.at[c], r2_ss.at[0, c], r2_rs.at[0, c], dev(me, yr, z)),
                remote(sl.at[c], rr.at[c], r2_ss.at[1, c], r2_rs.at[1, c], dev(me, yl, z)),
            )
            for cp in r2[c]:
                cp.start()
        c = i - 4
        if 0 <= c < NC:
            for cp in r2[c]:
                cp.wait_recv()
            total = part[c % 3, 0] + rl[c].astype(F32) + rr[c].astype(F32)
            out_ref[c * CR : (c + 1) * CR, :] = total.astype(BF)
    for c in range(NC):
        for cps in (ag[c], fw[c], r1[c], r2[c]):
            for cp in cps:
                cp.wait_send()


def on_device(streams, conv_weight, skip_weight, long_filter, out_weight):
    vm = pl.BlockSpec(memory_space=pltpu.VMEM)
    dma = pltpu.SemaphoreType.DMA
    return pl.pallas_call(
        kernel,
        out_shape=jax.ShapeDtypeStruct((ROWS, CH), BF),
        in_specs=[vm, vm, vm, vm, pl.BlockSpec(memory_space=pl.ANY)] + [vm] * 7,
        out_specs=vm,
        scratch_shapes=[
            pltpu.VMEM((3, 16, CH), BF),
            pltpu.VMEM((3, 8 + ROWS, CH), F32),
            pltpu.VMEM((ROWS, CH), F32),
            pltpu.VMEM((ROWS, CH), BF),
            pltpu.VMEM((TILES, CH, 128), BF),
            pltpu.VMEM((TILES, CH, 128), BF),
            pltpu.VMEM((NA, LC, 128), BF),
            pltpu.VMEM((NA, LC, 128), BF),
            pltpu.VMEM((NA * LC, 128), F32),
            pltpu.VMEM((GROUPS, 256, 256), F32),
            pltpu.VMEM((CTX, 512, 128), BF),
            pltpu.VMEM((CTX, 512, 128), BF),
            pltpu.VMEM((NY, NZ * CH, CH), BF),
            pltpu.VMEM((NZ, ROWS, CH), BF),
            pltpu.VMEM((NC, CR, CH), BF),
            pltpu.VMEM((NC, CR // 2, CH), BF),
            pltpu.VMEM((NC, CR // 2, CH), BF),
            pltpu.VMEM((NC, CR, CH), BF),
            pltpu.VMEM((NC, CR, CH), BF),
            pltpu.VMEM((NC, CR, CH), BF),
            pltpu.VMEM((NC, CR, CH), BF),
            pltpu.VMEM((3, 3, CR, CH), F32),
            dma((2,)),
            dma((7,)), dma((7,)), dma((1,)),
            dma((7,)), dma((7,)), dma((1,)),
            dma((7,)), dma((7,)), dma((1,)),
            dma((3, NY)), dma((3, NY)), dma((NY,)),
            dma((3, NY)), dma((3, NY)),
            dma((2, NC)), dma((2, NC)),
            dma((2, NC)), dma((2, NC)),
            dma((2, NC)), dma((2, NC)),
            dma((2, NC)), dma((2, NC)),
        ],
        compiler_params=pltpu.CompilerParams(
            collective_id=0, has_side_effects=True, vmem_limit_bytes=60 * 1024 * 1024
        ),
        name="hyena",
    )(streams, long_filter, conv_weight, skip_weight.reshape(1, CH), out_weight, *tables())


def solution(mesh):
    return jax.shard_map(
        on_device,
        mesh=mesh,
        in_specs=(
            P(None, "ctx", "tp"),
            P(None, None, "tp"),
            P("tp"),
            P("ctx", "tp"),
            P("tp", None),
        ),
        out_specs=P("ctx", "tp"),
        check_vma=False,
    )
```

```python
import functools
import math

import jax
import jax.numpy as jnp
import ml_dtypes
import numpy as np
from jax import lax
from jax.experimental import pallas as pl
from jax.experimental.pallas import tpu as pltpu
from jax.sharding import PartitionSpec as P

BF = jnp.bfloat16
F32 = jnp.float32
MESH = pl.DeviceIdType.MESH

ROWS = 1024
CH = 512
CTX = 8
NY = 4
NZ = 4
LC = CH // CTX
LH = LC // 2
WQ = CH // 8
TILES = ROWS // 128
NA = 64
GROUPS = LC // 4
NC = 8
CR = ROWS // NC
ORDER = (
    *"goowgofgfgofvmmorfrmofemoefrmrofmerfmermereree",
)
QS = 4


def tables():
    k1 = np.arange(64) + 0.25
    a = np.arange(64)
    b = np.arange(128)
    th1 = 2 * np.pi * np.outer(k1, a) / 64
    c1, s1 = np.cos(th1), np.sin(th1)
    eye = np.eye(4)
    f1 = np.concatenate([np.kron(eye, c1), np.kron(eye, s1)], axis=0)
    th2 = 2 * np.pi * np.outer(b, b) / 128
    c2, s2 = np.cos(th2), np.sin(th2)
    f2 = np.block([[c2, s2], [-s2, c2]])
    f2i = np.block([[c2, -s2], [s2, c2]])
    inv = np.concatenate([np.kron(eye, c1.T), np.kron(eye, s1.T)], axis=1) / 8192.0
    inv = inv.reshape(4, 8, 4, 2, 512).transpose(2, 1, 0, 3, 4).reshape(256, 512)
    tw = 2 * np.pi * np.outer(k1, b) / 8192
    twc, tws = np.tile(np.cos(tw), (4, 1)), np.tile(np.sin(tw), (4, 1))
    bf = lambda m: jnp.asarray(m.astype(np.float32).astype(ml_dtypes.bfloat16))
    return (
        bf(f1),
        bf(f2),
        bf(f2i),
        bf(inv),
        jnp.asarray(twc.astype(np.float32)),
        jnp.asarray(tws.astype(np.float32)),
    )


def nt(a, b):
    return lax.dot_general(a, b, (((1,), (1,)), ((), ())), preferred_element_type=F32)


def mm(a, b):
    return jnp.dot(a, b, preferred_element_type=F32)


def kernel(
    x_ref, h_ref, cw_ref, skip_ref, w_ref, f1_ref, f2_ref, f2i_ref, f1i_ref, twc_ref, tws_ref,
    out_ref,
    xv, hv, tb1, tb2, tb3, tb4, tb5, tb6, outv, halo, x32, gat, upos, sh, su, rh, ru, r32, spec, ys, ry, wr, gall, sopp, ra, rb, sl, sr, rl, rr, part,
    in_sem, out_sem, halo_sem, h_ss, h_rs, h_ls, u_ss, u_rs, u_ls, y_ss, y_rs, y_ls,
    w_ss, w_rs, w_ls, f_ss, f_rs, x_ss, x_rs, ag_ss, ag_rs, fw_ss, fw_rs, r1_ss, r1_rs, r2_ss, r2_rs,
):
    me = lax.axis_index("ctx")
    tp = lax.axis_index("tp")
    y = tp // NZ
    z = tp % NZ
    core = me % 2
    sib = me + 1 - 2 * core

    def dev(ctx, yy, zz):
        return (ctx, yy * NZ + zz)

    def remote(src, dst, ss, rs, to):
        return pltpu.make_async_remote_copy(
            src_ref=src, dst_ref=dst, send_sem=ss, recv_sem=rs, device_id=to, device_id_type=MESH
        )

    ins = [
        pltpu.make_async_copy(src, dst, in_sem.at[k])
        for k, (src, dst) in enumerate(
            [(h_ref, hv), (x_ref.at[1], xv.at[1]), (x_ref.at[2], xv.at[2]), (x_ref.at[0], xv.at[0]),
             (f1_ref, tb1), (f2_ref, tb2), (f2i_ref, tb3), (f1i_ref, tb4), (twc_ref, tb5), (tws_ref, tb6)]
        )
    ]
    for cp in ins:
        cp.start()

    barrier = pltpu.get_barrier_semaphore()
    for d in range(1, CTX):
        pl.semaphore_signal(barrier, inc=1, device_id=dev((me + d) % CTX, y, z), device_id_type=MESH)
    for d in range(1, NZ):
        pl.semaphore_signal(barrier, inc=1, device_id=dev(me, y, (z + d) % NZ), device_id_type=MESH)
    for d in (1, 3):
        pl.semaphore_signal(barrier, inc=1, device_id=dev(me, (y + d) % NY, z), device_id_type=MESH)
    pl.semaphore_wait(barrier, 12)

    halo_cp = remote(
        x_ref.at[:, ROWS - 16 :, :], halo, halo_sem.at[0], halo_sem.at[1], dev((me + 1) % CTX, y, z)
    )
    halo_cp.start()

    half = pl.multiple_of(core * (CH // 2), CH // 2)
    w_cps = {}
    quarter = pl.multiple_of(half + (me // 2) * WQ, WQ)
    for d in (2, 1, 3):
        zp = (z + d) % NZ
        first, count = (quarter, WQ) if d == 2 else (half, CH // 2)
        for k in range(NY):
            yb = (y + k) % NY
            cols = pl.multiple_of((NZ * yb + zp) * CH, CH)
            w_cps[d, k] = remote(
                w_ref.at[pl.ds(first, count), pl.ds(cols, CH)],
                wr.at[yb, pl.ds(z * CH + first, count), :],
                w_ss.at[d - 1, k],
                w_rs.at[d - 1, k],
                dev(me, y, zp),
            )
    for cp in w_cps.values():
        cp.start()
    w_local = []
    for yb in range(NY):
        cols = pl.multiple_of((NZ * yb + z) * CH, CH)
        w_local.append(
            pltpu.make_async_copy(w_ref.at[:, pl.ds(cols, CH)], wr.at[yb, pl.ds(z * CH, CH), :], w_ls.at[yb])
        )
    for cp in w_local:
        cp.start()

    def exchange(send, recv, ss, rs, ls):
        both = []
        for h in range(2):
            cps = []
            for d in (4, 3, 5, 2, 6, 1, 7):
                j = (me + d) % CTX
                cps.append(
                    remote(
                        send.at[:, pl.ds(pl.multiple_of(j * LC + h * LH, LH), LH), :],
                        recv.at[h, pl.ds(me * TILES, TILES)],
                        ss.at[h, d - 1],
                        rs.at[h, d - 1],
                        dev(j, y, z),
                    )
                )
            cps.append(
                pltpu.make_async_copy(
                    send.at[:, pl.ds(pl.multiple_of(me * LC + h * LH, LH), LH), :],
                    recv.at[h, pl.ds(me * TILES, TILES)],
                    ls.at[h],
                )
            )
            both.append(cps)
        return both

    eye = (
        lax.broadcasted_iota(jnp.int32, (256, 256), 0) == lax.broadcasted_iota(jnp.int32, (256, 256), 1)
    ).astype(F32).astype(BF)
    ins[0].wait()
    for t in range(TILES):
        for q in range(CH // 256):
            sh[t, 256 * q : 256 * q + 256, :] = nt(
                eye, hv[128 * t : 128 * t + 128, 256 * q : 256 * q + 256]
            ).astype(BF)
    h_cps = exchange(sh, rh, h_ss, h_rs, h_ls)
    for cp in h_cps[0] + h_cps[1]:
        cp.start()

    for k, s in ((1, 1), (2, 2), (3, 0)):
        ins[k].wait()
        x32[s, 8:, :] = xv[s].astype(F32)
    halo_cp.wait()
    edge = halo[...].astype(F32)[:, 8:16, :]
    x32[:, 0:8, :] = jnp.where(me == 0, jnp.zeros_like(edge), edge)

    def short(s, t, q):
        cs = slice(256 * q, 256 * q + 256)
        base = 8 + 128 * t
        acc = cw_ref[s, 0:1, cs] * x32[s, base : base + 128, cs]
        acc = acc + cw_ref[s, 1:2, cs] * x32[s, base - 1 : base + 127, cs]
        return acc + cw_ref[s, 2:3, cs] * x32[s, base - 2 : base + 126, cs]

    for t in range(TILES):
        for q in range(CH // 256):
            u = (short(1, t, q) * short(2, t, q)).astype(BF)
            upos[128 * t : 128 * t + 128, 256 * q : 256 * q + 256] = u
            su[t, 256 * q : 256 * q + 256, :] = nt(eye, u).astype(BF)
    u_cps = exchange(su, ru, u_ss, u_rs, u_ls)
    for cp in u_cps[0] + u_cps[1]:
        cp.start()

    for t in range(TILES):
        for q in range(CH // 256):
            gat[128 * t : 128 * t + 128, 256 * q : 256 * q + 256] = short(0, t, q)

    for cp in ins[4:]:
        cp.wait()

    def load_group(h, g):
        rows = [r32[h, pl.ds(4 * g + i, NA, stride=LH), :] for i in range(4)]
        return jnp.concatenate(rows, axis=0).astype(BF)

    def forward(v):
        o = mm(tb1[...], v)
        re, im = o[:256], o[256:]
        c, s = tb5[...], tb6[...]
        lhs = jnp.concatenate([(re * c - im * s).astype(BF), (re * s + im * c).astype(BF)], axis=1)
        return mm(lhs, tb2[...])

    for h in range(2):
        for cp in h_cps[h]:
            cp.wait()
        r32[h] = rh[h].astype(F32).reshape(NA * LH, 128)

        def filter_group(g, carry, h=h):
            spec[h * (GROUPS // 2) + g] = forward(load_group(h, g))
            return carry

        lax.fori_loop(0, GROUPS // 2, filter_group, 0)

    opp = pl.multiple_of(((z + 2) % NZ) * CH + quarter, WQ)
    x_cps = {}

    def line(ks):
        for k in ks:
            blk = wr.at[(y + k) % NY, pl.ds(opp, WQ), :]
            w_cps[2, k].wait()
            for n in range(1, 4):
                to = dev((me + 2 * n) % CTX, y, z)
                x_cps[k, n] = remote(blk, blk, x_ss.at[k, n - 1], x_rs.at[k, n - 1], to)
                x_cps[k, n].start()

    def signal_group(h, g):
        o = forward(load_group(h, g))
        f = spec[h * (GROUPS // 2) + g]
        ur, ui = o[:, :128], o[:, 128:]
        hr, hi = f[:, :128], f[:, 128:]
        lhs = jnp.concatenate([(ur * hr - ui * hi).astype(BF), (ur * hi + ui * hr).astype(BF)], axis=1)
        v = mm(lhs, tb3[...])
        vr, vi = v[:, :128], v[:, 128:]
        c, s = tb5[...], tb6[...]
        return jnp.concatenate([(vr * c + vi * s).astype(BF), (vi * c - vr * s).astype(BF)], axis=0)

    for h in range(2):
        for cp in u_cps[h]:
            cp.wait()
        if h == 1:
            line((2, 1))
        r32[h] = ru[h].astype(F32).reshape(NA * LH, 128)

        def signal_pair(i, carry, h=h):
            v = jnp.concatenate([signal_group(h, 2 * i), signal_group(h, 2 * i + 1)], axis=1)
            o = mm(tb4[...], v)
            o = jnp.concatenate([o[:, :128].reshape(32, 8, 128), o[:, 128:].reshape(32, 8, 128)], axis=1)
            at = pl.multiple_of(16 * (h * (GROUPS // 4) + i), 16)
            ys[:, :, pl.ds(at, 16), :] = o.reshape(QS, CTX, 16, 128).astype(BF)
            return carry

        lax.fori_loop(0, GROUPS // 4, signal_pair, 0)

    y_cps = []
    for q in range(QS):
        cps = []
        for d in (4, 3, 5, 2, 6, 1, 7):
            j = (me + d) % CTX
            cps.append(remote(ys.at[q, j], ry.at[q, me], y_ss.at[q, d - 1], y_rs.at[q, d - 1], dev(j, y, z)))
        cps.append(pltpu.make_async_copy(ys.at[q, me], ry.at[q, me], y_ls.at[q]))
        for cp in cps:
            cp.start()
        if q == 0:
            line((3, 0))
        y_cps.append(cps)
    eye128 = eye[0:128, 0:128]

    def gate(q):
        for cp in y_cps[q]:
            cp.wait()
        r32[q // 2, 1024 * (q % 2) : 1024 * (q % 2) + 1024, :] = ry[q].astype(F32).reshape(1024, 128)
        for k in range(2):
            long_out = nt(eye128, r32[q // 2, pl.ds(1024 * (q % 2) + k, CH, stride=2), :].astype(BF))
            rows = slice(256 * q + 128 * k, 256 * q + 128 * k + 128)
            gated = (long_out + skip_ref[...] * upos[rows, :].astype(F32)) * gat[rows, :]
            gall[z, rows, :] = gated.astype(BF)

    f_cps = {}

    def share(d):
        blk = wr.at[:, pl.ds(pl.multiple_of(((z + NZ - d) % NZ) * CH + half, CH // 2), CH // 2), :]
        f_cps[d] = remote(blk, blk, f_ss.at[d - 1], f_rs.at[d - 1], dev(sib, y, z))
        f_cps[d].start()

    def weights(step):
        if step == 0:
            for d in (1, 3):
                for k in range(NY):
                    w_cps[d, k].wait()
                share(d)
        else:
            for cp in x_cps.values():
                cp.wait()
            share(2)
            for cp in w_local:
                cp.wait()
            for cp in f_cps.values():
                cp.wait()

    zl, zr, zo = (z + 3) % NZ, (z + 1) % NZ, (z + 2) % NZ
    yl, yr, yo = (y + 3) % NY, (y + 1) % NY, (y + 2) % NY
    hr_ = CR // 2
    ag, fw, r1, r2, oc = {}, {}, {}, {}, {}

    def own(c):
        blk = gall.at[z, c * CR : (c + 1) * CR, :]
        ag[c] = (
            remote(blk, blk, ag_ss.at[0, c], ag_rs.at[0, c], dev(me, y, zr)),
            remote(blk, blk, ag_ss.at[1, c], ag_rs.at[1, c], dev(me, y, zl)),
        )
        for cp in ag[c]:
            cp.start()

    def pass_on(c):
        up = gall.at[zl, c * CR : c * CR + hr_, :]
        dn = gall.at[zr, c * CR + hr_ : (c + 1) * CR, :]
        fw[c] = (
            remote(up, up, fw_ss.at[0, c], fw_rs.at[0, c], dev(me, y, zr)),
            remote(dn, dn, fw_ss.at[1, c], fw_rs.at[1, c], dev(me, y, zl)),
        )
        for k in range(2):
            ag[c][k].wait_recv()
            fw[c][k].start()

    def multiply(c):
        for k in range(2):
            fw[c][k].wait_recv()

        def product(yb):
            acc = mm(gall[0, c * CR : (c + 1) * CR, :], wr[yb, 0:CH, :])
            for k in range(1, NZ):
                acc = acc + mm(gall[k, c * CR : (c + 1) * CR, :], wr[yb, k * CH : (k + 1) * CH, :])
            return acc

        sopp[c] = product(yo).astype(BF)
        r1[c] = (
            remote(sopp.at[c, 0:hr_, :], ra.at[c], r1_ss.at[0, c], r1_rs.at[0, c], dev(me, yr, z)),
            remote(sopp.at[c, hr_:CR, :], rb.at[c], r1_ss.at[1, c], r1_rs.at[1, c], dev(me, yl, z)),
        )
        for cp in r1[c]:
            cp.start()
        part[c, 1] = product(yr)
        part[c, 2] = product(yl)
        part[c, 0] = product(y)

    def reduce(c):
        r1[c][0].wait_recv()
        sr[c, 0:hr_, :] = (part[c, 1, 0:hr_, :] + ra[c].astype(F32)).astype(BF)
        sr[c, hr_:CR, :] = part[c, 1, hr_:CR, :].astype(BF)
        r1[c][1].wait_recv()
        sl[c, hr_:CR, :] = (part[c, 2, hr_:CR, :] + rb[c].astype(F32)).astype(BF)
        sl[c, 0:hr_, :] = part[c, 2, 0:hr_, :].astype(BF)
        r2[c] = (
            remote(sr.at[c], rl.at[c], r2_ss.at[0, c], r2_rs.at[0, c], dev(me, yr, z)),
            remote(sl.at[c], rr.at[c], r2_ss.at[1, c], r2_rs.at[1, c], dev(me, yl, z)),
        )
        for cp in r2[c]:
            cp.start()

    def end(c):
        for cp in r2[c]:
            cp.wait_recv()
        total = part[c, 0] + rl[c].astype(F32) + rr[c].astype(F32)
        outv[c * CR : (c + 1) * CR, :] = total.astype(BF)
        oc[c] = pltpu.make_async_copy(
            outv.at[c * CR : (c + 1) * CR, :], out_ref.at[c * CR : (c + 1) * CR, :], out_sem.at[c]
        )
        oc[c].start()

    steps = dict(g=gate, o=own, f=pass_on, w=weights, m=multiply, r=reduce, e=end)
    count = dict.fromkeys(steps, 0)
    for k in ORDER:
        k = "w" if k == "v" else k
        steps[k](count[k])
        count[k] += 1
    for c in range(NC):
        for cps in (ag[c], fw[c], r1[c], r2[c]):
            for cp in cps:
                cp.wait_send()
        oc[c].wait()


def on_device(streams, conv_weight, skip_weight, long_filter, out_weight):
    vm = pl.BlockSpec(memory_space=pltpu.VMEM)
    hbm = pl.BlockSpec(memory_space=pl.ANY)
    dma = pltpu.SemaphoreType.DMA
    return pl.pallas_call(
        kernel,
        out_shape=jax.ShapeDtypeStruct((ROWS, CH), BF),
        in_specs=[hbm, hbm, vm, vm] + [hbm] * 7,
        out_specs=hbm,
        scratch_shapes=[
            pltpu.VMEM((3, ROWS, CH), BF),
            pltpu.VMEM((ROWS, CH), BF),
            pltpu.VMEM((512, 256), BF),
            pltpu.VMEM((256, 256), BF),
            pltpu.VMEM((256, 256), BF),
            pltpu.VMEM((256, 512), BF),
            pltpu.VMEM((256, 128), F32),
            pltpu.VMEM((256, 128), F32),
            pltpu.VMEM((ROWS, CH), BF),
            pltpu.VMEM((3, 16, CH), BF),
            pltpu.VMEM((3, 8 + ROWS, CH), F32),
            pltpu.VMEM((ROWS, CH), F32),
            pltpu.VMEM((ROWS, CH), BF),
            pltpu.VMEM((TILES, CH, 128), BF),
            pltpu.VMEM((TILES, CH, 128), BF),
            pltpu.VMEM((2, NA, LH, 128), BF),
            pltpu.VMEM((2, NA, LH, 128), BF),
            pltpu.VMEM((2, NA * LH, 128), F32),
            pltpu.VMEM((GROUPS, 256, 256), F32),
            pltpu.VMEM((QS, CTX, 128, 128), BF),
            pltpu.VMEM((QS, CTX, 128, 128), BF),
            pltpu.VMEM((NY, NZ * CH, CH), BF),
            pltpu.VMEM((NZ, ROWS, CH), BF),
            pltpu.VMEM((NC, CR, CH), BF),
            pltpu.VMEM((NC, CR // 2, CH), BF),
            pltpu.VMEM((NC, CR // 2, CH), BF),
            pltpu.VMEM((NC, CR, CH), BF),
            pltpu.VMEM((NC, CR, CH), BF),
            pltpu.VMEM((NC, CR, CH), BF),
            pltpu.VMEM((NC, CR, CH), BF),
            pltpu.VMEM((NC, 3, CR, CH), F32),
            dma((10,)),
            dma((NC,)),
            dma((2,)),
            dma((2, 7)), dma((2, 7)), dma((2,)),
            dma((2, 7)), dma((2, 7)), dma((2,)),
            dma((QS, 7)), dma((QS, 7)), dma((QS,)),
            dma((3, NY)), dma((3, NY)), dma((NY,)),
            dma((3,)), dma((3,)), dma((NY, 3)), dma((NY, 3)),
            dma((2, NC)), dma((2, NC)),
            dma((2, NC)), dma((2, NC)),
            dma((2, NC)), dma((2, NC)),
            dma((2, NC)), dma((2, NC)),
        ],
        compiler_params=pltpu.CompilerParams(
            collective_id=0, has_side_effects=True, vmem_limit_bytes=60 * 1024 * 1024
        ),
        name="hyena",
    )(streams, long_filter, conv_weight, skip_weight.reshape(1, CH), out_weight, *tables())


def solution(mesh):
    return jax.shard_map(
        on_device,
        mesh=mesh,
        in_specs=(
            P(None, "ctx", "tp"),
            P(None, None, "tp"),
            P("tp"),
            P("ctx", "tp"),
            P("tp", None),
        ),
        out_specs=P("ctx", "tp"),
        check_vma=False,
    )
```

```python
import functools
import math

import jax
import jax.numpy as jnp
import ml_dtypes
import numpy as np
from jax import lax
from jax.experimental import pallas as pl
from jax.experimental.pallas import tpu as pltpu
from jax.sharding import PartitionSpec as P

BF = jnp.bfloat16
F32 = jnp.float32
MESH = pl.DeviceIdType.MESH

ROWS = 1024
CH = 512
CTX = 8
NY = 4
NZ = 4
LC = CH // CTX
LH = LC // 2
WQ = CH // 8
TILES = ROWS // 128
NA = 64
GROUPS = LC // 4
NC = 8
CR = ROWS // NC
LINE = (2, 1)
ORDER = (
    *"goowgofgfgofvmmorfrmofemoefrmrofmerfmermereree",
)
QS = 4


def tables():
    k1 = np.arange(64) + 0.25
    a = np.arange(64)
    b = np.arange(128)
    th1 = 2 * np.pi * np.outer(k1, a) / 64
    c1, s1 = np.cos(th1), np.sin(th1)
    eye = np.eye(4)
    f1 = np.concatenate([np.kron(eye, c1), np.kron(eye, s1)], axis=0)
    th2 = 2 * np.pi * np.outer(b, b) / 128
    c2, s2 = np.cos(th2), np.sin(th2)
    f2 = np.block([[c2, s2], [-s2, c2]])
    f2i = np.block([[c2, -s2], [s2, c2]])
    inv = np.concatenate([np.kron(eye, c1.T), np.kron(eye, s1.T)], axis=1) / 8192.0
    inv = inv.reshape(4, 8, 4, 2, 512).transpose(2, 1, 0, 3, 4).reshape(256, 512)
    tw = 2 * np.pi * np.outer(k1, b) / 8192
    twc, tws = np.tile(np.cos(tw), (4, 1)), np.tile(np.sin(tw), (4, 1))
    bf = lambda m: jnp.asarray(m.astype(np.float32).astype(ml_dtypes.bfloat16))
    return (
        bf(f1),
        bf(f2),
        bf(f2i),
        bf(inv),
        jnp.asarray(twc.astype(np.float32)),
        jnp.asarray(tws.astype(np.float32)),
    )


def nt(a, b):
    return lax.dot_general(a, b, (((1,), (1,)), ((), ())), preferred_element_type=F32)


def mm(a, b):
    return jnp.dot(a, b, preferred_element_type=F32)


def kernel(
    x_ref, h_ref, cw_ref, skip_ref, w_ref, f1_ref, f2_ref, f2i_ref, f1i_ref, twc_ref, tws_ref,
    out_ref,
    xv, hv, tb1, tb2, tb3, tb4, tb5, tb6, outv, halo, x32, gat, upos, sh, su, rh, ru, r32, spec, ys, ry, wr, gall, sopp, ra, rb, sl, sr, rl, rr, part,
    in_sem, out_sem, halo_sem, h_ss, h_rs, h_ls, u_ss, u_rs, u_ls, y_ss, y_rs, y_ls,
    w_ss, w_rs, w_ls, f_ss, f_rs, x_ss, x_rs, ag_ss, ag_rs, fw_ss, fw_rs, r1_ss, r1_rs, r2_ss, r2_rs,
):
    me = lax.axis_index("ctx")
    tp = lax.axis_index("tp")
    y = tp // NZ
    z = tp % NZ
    core = me % 2
    sib = me + 1 - 2 * core

    def dev(ctx, yy, zz):
        return (ctx, yy * NZ + zz)

    def remote(src, dst, ss, rs, to):
        return pltpu.make_async_remote_copy(
            src_ref=src, dst_ref=dst, send_sem=ss, recv_sem=rs, device_id=to, device_id_type=MESH
        )

    ins = [
        pltpu.make_async_copy(src, dst, in_sem.at[k])
        for k, (src, dst) in enumerate(
            [(h_ref, hv), (x_ref.at[1], xv.at[1]), (x_ref.at[2], xv.at[2]), (x_ref.at[0], xv.at[0]),
             (f1_ref, tb1), (f2_ref, tb2), (f2i_ref, tb3), (f1i_ref, tb4), (twc_ref, tb5), (tws_ref, tb6)]
        )
    ]
    for cp in ins:
        cp.start()

    barrier = pltpu.get_barrier_semaphore()
    for d in range(1, CTX):
        pl.semaphore_signal(barrier, inc=1, device_id=dev((me + d) % CTX, y, z), device_id_type=MESH)
    for d in range(1, NZ):
        pl.semaphore_signal(barrier, inc=1, device_id=dev(me, y, (z + d) % NZ), device_id_type=MESH)
    for d in (1, 3):
        pl.semaphore_signal(barrier, inc=1, device_id=dev(me, (y + d) % NY, z), device_id_type=MESH)
    pl.semaphore_wait(barrier, 12)

    halo_cp = remote(
        x_ref.at[:, ROWS - 16 :, :], halo, halo_sem.at[0], halo_sem.at[1], dev((me + 1) % CTX, y, z)
    )
    halo_cp.start()

    half = pl.multiple_of(core * (CH // 2), CH // 2)
    w_cps = {}
    quarter = pl.multiple_of(half + (me // 2) * WQ, WQ)
    for d in (2, 1, 3):
        zp = (z + d) % NZ
        for k in range(NY):
            first, count = (quarter, WQ) if d == 2 and k in LINE else (half, CH // 2)
            yb = (y + k) % NY
            cols = pl.multiple_of((NZ * yb + zp) * CH, CH)
            w_cps[d, k] = remote(
                w_ref.at[pl.ds(first, count), pl.ds(cols, CH)],
                wr.at[yb, pl.ds(z * CH + first, count), :],
                w_ss.at[d - 1, k],
                w_rs.at[d - 1, k],
                dev(me, y, zp),
            )
    for cp in w_cps.values():
        cp.start()
    w_local = []
    for yb in range(NY):
        cols = pl.multiple_of((NZ * yb + z) * CH, CH)
        w_local.append(
            pltpu.make_async_copy(w_ref.at[:, pl.ds(cols, CH)], wr.at[yb, pl.ds(z * CH, CH), :], w_ls.at[yb])
        )
    for cp in w_local:
        cp.start()

    def exchange(send, recv, ss, rs, ls):
        both = []
        for h in range(2):
            cps = []
            for d in (4, 3, 5, 2, 6, 1, 7):
                j = (me + d) % CTX
                cps.append(
                    remote(
                        send.at[:, pl.ds(pl.multiple_of(j * LC + h * LH, LH), LH), :],
                        recv.at[h, pl.ds(me * TILES, TILES)],
                        ss.at[h, d - 1],
                        rs.at[h, d - 1],
                        dev(j, y, z),
                    )
                )
            cps.append(
                pltpu.make_async_copy(
                    send.at[:, pl.ds(pl.multiple_of(me * LC + h * LH, LH), LH), :],
                    recv.at[h, pl.ds(me * TILES, TILES)],
                    ls.at[h],
                )
            )
            both.append(cps)
        return both

    eye = (
        lax.broadcasted_iota(jnp.int32, (256, 256), 0) == lax.broadcasted_iota(jnp.int32, (256, 256), 1)
    ).astype(F32).astype(BF)
    ins[0].wait()
    for t in range(TILES):
        for q in range(CH // 256):
            sh[t, 256 * q : 256 * q + 256, :] = nt(
                eye, hv[128 * t : 128 * t + 128, 256 * q : 256 * q + 256]
            ).astype(BF)
    h_cps = exchange(sh, rh, h_ss, h_rs, h_ls)
    for cp in h_cps[0] + h_cps[1]:
        cp.start()

    for k in (1, 2):
        ins[k].wait()
        x32[k, 8:, :] = xv[k].astype(F32)
    halo_cp.wait()
    edge = halo[...].astype(F32)[:, 8:16, :]
    x32[:, 0:8, :] = jnp.where(me == 0, jnp.zeros_like(edge), edge)

    def short(s, t, q):
        cs = slice(256 * q, 256 * q + 256)
        base = 8 + 128 * t
        acc = cw_ref[s, 0:1, cs] * x32[s, base : base + 128, cs]
        acc = acc + cw_ref[s, 1:2, cs] * x32[s, base - 1 : base + 127, cs]
        return acc + cw_ref[s, 2:3, cs] * x32[s, base - 2 : base + 126, cs]

    for t in range(TILES):
        for q in range(CH // 256):
            u = (short(1, t, q) * short(2, t, q)).astype(BF)
            upos[128 * t : 128 * t + 128, 256 * q : 256 * q + 256] = u
            su[t, 256 * q : 256 * q + 256, :] = nt(eye, u).astype(BF)
    u_cps = exchange(su, ru, u_ss, u_rs, u_ls)
    for cp in u_cps[0] + u_cps[1]:
        cp.start()

    ins[3].wait()
    x32[0, 8:, :] = xv[0].astype(F32)

    for t in range(TILES):
        for q in range(CH // 256):
            gat[128 * t : 128 * t + 128, 256 * q : 256 * q + 256] = short(0, t, q)

    for cp in ins[4:]:
        cp.wait()

    def load_group(h, g):
        rows = [r32[h, pl.ds(4 * g + i, NA, stride=LH), :] for i in range(4)]
        return jnp.concatenate(rows, axis=0).astype(BF)

    def forward(v):
        o = mm(tb1[...], v)
        re, im = o[:256], o[256:]
        c, s = tb5[...], tb6[...]
        lhs = jnp.concatenate([(re * c - im * s).astype(BF), (re * s + im * c).astype(BF)], axis=1)
        return mm(lhs, tb2[...])

    for h in range(2):
        for cp in h_cps[h]:
            cp.wait()
        r32[h] = rh[h].astype(F32).reshape(NA * LH, 128)

        def filter_group(g, carry, h=h):
            spec[h * (GROUPS // 2) + g] = forward(load_group(h, g))
            return carry

        lax.fori_loop(0, GROUPS // 2, filter_group, 0)

    opp = pl.multiple_of(((z + 2) % NZ) * CH + quarter, WQ)
    x_cps = {}

    def line():
        for k in LINE:
            blk = wr.at[(y + k) % NY, pl.ds(opp, WQ), :]
            w_cps[2, k].wait()
            for n in range(1, 4):
                to = dev((me + 2 * n) % CTX, y, z)
                x_cps[k, n] = remote(blk, blk, x_ss.at[k, n - 1], x_rs.at[k, n - 1], to)
                x_cps[k, n].start()

    def signal_group(h, g):
        o = forward(load_group(h, g))
        f = spec[h * (GROUPS // 2) + g]
        ur, ui = o[:, :128], o[:, 128:]
        hr, hi = f[:, :128], f[:, 128:]
        lhs = jnp.concatenate([(ur * hr - ui * hi).astype(BF), (ur * hi + ui * hr).astype(BF)], axis=1)
        v = mm(lhs, tb3[...])
        vr, vi = v[:, :128], v[:, 128:]
        c, s = tb5[...], tb6[...]
        return jnp.concatenate([(vr * c + vi * s).astype(BF), (vi * c - vr * s).astype(BF)], axis=0)

    for h in range(2):
        for cp in u_cps[h]:
            cp.wait()
        if h == 1:
            line()
        r32[h] = ru[h].astype(F32).reshape(NA * LH, 128)

        def signal_pair(i, carry, h=h):
            v = jnp.concatenate([signal_group(h, 2 * i), signal_group(h, 2 * i + 1)], axis=1)
            o = mm(tb4[...], v)
            o = jnp.concatenate([o[:, :128].reshape(32, 8, 128), o[:, 128:].reshape(32, 8, 128)], axis=1)
            at = pl.multiple_of(16 * (h * (GROUPS // 4) + i), 16)
            ys[:, :, pl.ds(at, 16), :] = o.reshape(QS, CTX, 16, 128).astype(BF)
            return carry

        lax.fori_loop(0, GROUPS // 4, signal_pair, 0)

    y_cps = []
    for q in range(QS):
        cps = []
        for d in (4, 3, 5, 2, 6, 1, 7):
            j = (me + d) % CTX
            cps.append(remote(ys.at[q, j], ry.at[q, me], y_ss.at[q, d - 1], y_rs.at[q, d - 1], dev(j, y, z)))
        cps.append(pltpu.make_async_copy(ys.at[q, me], ry.at[q, me], y_ls.at[q]))
        for cp in cps:
            cp.start()
        y_cps.append(cps)
    eye128 = eye[0:128, 0:128]

    def gate(q):
        for cp in y_cps[q]:
            cp.wait()
        r32[q // 2, 1024 * (q % 2) : 1024 * (q % 2) + 1024, :] = ry[q].astype(F32).reshape(1024, 128)
        for k in range(2):
            long_out = nt(eye128, r32[q // 2, pl.ds(1024 * (q % 2) + k, CH, stride=2), :].astype(BF))
            rows = slice(256 * q + 128 * k, 256 * q + 128 * k + 128)
            gated = (long_out + skip_ref[...] * upos[rows, :].astype(F32)) * gat[rows, :]
            gall[z, rows, :] = gated.astype(BF)

    f_cps = {}

    def share(d):
        blk = wr.at[:, pl.ds(pl.multiple_of(((z + NZ - d) % NZ) * CH + half, CH // 2), CH // 2), :]
        f_cps[d] = remote(blk, blk, f_ss.at[d - 1], f_rs.at[d - 1], dev(sib, y, z))
        f_cps[d].start()

    def weights(step):
        if step == 0:
            for d in (1, 3):
                for k in range(NY):
                    w_cps[d, k].wait()
                share(d)
        else:
            for k in range(NY):
                if k not in LINE:
                    w_cps[2, k].wait()
            for cp in x_cps.values():
                cp.wait()
            share(2)
            for cp in w_local:
                cp.wait()
            for cp in f_cps.values():
                cp.wait()

    zl, zr, zo = (z + 3) % NZ, (z + 1) % NZ, (z + 2) % NZ
    yl, yr, yo = (y + 3) % NY, (y + 1) % NY, (y + 2) % NY
    hr_ = CR // 2
    ag, fw, r1, r2, oc = {}, {}, {}, {}, {}

    def own(c):
        blk = gall.at[z, c * CR : (c + 1) * CR, :]
        ag[c] = (
            remote(blk, blk, ag_ss.at[0, c], ag_rs.at[0, c], dev(me, y, zr)),
            remote(blk, blk, ag_ss.at[1, c], ag_rs.at[1, c], dev(me, y, zl)),
        )
        for cp in ag[c]:
            cp.start()

    def pass_on(c):
        up = gall.at[zl, c * CR : c * CR + hr_, :]
        dn = gall.at[zr, c * CR + hr_ : (c + 1) * CR, :]
        fw[c] = (
            remote(up, up, fw_ss.at[0, c], fw_rs.at[0, c], dev(me, y, zr)),
            remote(dn, dn, fw_ss.at[1, c], fw_rs.at[1, c], dev(me, y, zl)),
        )
        for k in range(2):
            ag[c][k].wait_recv()
            fw[c][k].start()

    def multiply(c):
        for k in range(2):
            fw[c][k].wait_recv()

        def product(yb):
            acc = mm(gall[0, c * CR : (c + 1) * CR, :], wr[yb, 0:CH, :])
            for k in range(1, NZ):
                acc = acc + mm(gall[k, c * CR : (c + 1) * CR, :], wr[yb, k * CH : (k + 1) * CH, :])
            return acc

        sopp[c] = product(yo).astype(BF)
        r1[c] = (
            remote(sopp.at[c, 0:hr_, :], ra.at[c], r1_ss.at[0, c], r1_rs.at[0, c], dev(me, yr, z)),
            remote(sopp.at[c, hr_:CR, :], rb.at[c], r1_ss.at[1, c], r1_rs.at[1, c], dev(me, yl, z)),
        )
        for cp in r1[c]:
            cp.start()
        part[c, 1] = product(yr)
        part[c, 2] = product(yl)
        part[c, 0] = product(y)

    def reduce(c):
        r1[c][0].wait_recv()
        sr[c, 0:hr_, :] = (part[c, 1, 0:hr_, :] + ra[c].astype(F32)).astype(BF)
        sr[c, hr_:CR, :] = part[c, 1, hr_:CR, :].astype(BF)
        r1[c][1].wait_recv()
        sl[c, hr_:CR, :] = (part[c, 2, hr_:CR, :] + rb[c].astype(F32)).astype(BF)
        sl[c, 0:hr_, :] = part[c, 2, 0:hr_, :].astype(BF)
        r2[c] = (
            remote(sr.at[c], rl.at[c], r2_ss.at[0, c], r2_rs.at[0, c], dev(me, yr, z)),
            remote(sl.at[c], rr.at[c], r2_ss.at[1, c], r2_rs.at[1, c], dev(me, yl, z)),
        )
        for cp in r2[c]:
            cp.start()

    def end(c):
        for cp in r2[c]:
            cp.wait_recv()
        total = part[c, 0] + rl[c].astype(F32) + rr[c].astype(F32)
        outv[c * CR : (c + 1) * CR, :] = total.astype(BF)
        oc[c] = pltpu.make_async_copy(
            outv.at[c * CR : (c + 1) * CR, :], out_ref.at[c * CR : (c + 1) * CR, :], out_sem.at[c]
        )
        oc[c].start()

    steps = dict(g=gate, o=own, f=pass_on, w=weights, m=multiply, r=reduce, e=end)
    count = dict.fromkeys(steps, 0)
    for k in ORDER:
        k = "w" if k == "v" else k
        steps[k](count[k])
        count[k] += 1
    for c in range(NC):
        for cps in (ag[c], fw[c], r1[c], r2[c]):
            for cp in cps:
                cp.wait_send()
        oc[c].wait()


def on_device(streams, conv_weight, skip_weight, long_filter, out_weight):
    vm = pl.BlockSpec(memory_space=pltpu.VMEM)
    hbm = pl.BlockSpec(memory_space=pl.ANY)
    dma = pltpu.SemaphoreType.DMA
    return pl.pallas_call(
        kernel,
        out_shape=jax.ShapeDtypeStruct((ROWS, CH), BF),
        in_specs=[hbm, hbm, vm, vm] + [hbm] * 7,
        out_specs=hbm,
        scratch_shapes=[
            pltpu.VMEM((3, ROWS, CH), BF),
            pltpu.VMEM((ROWS, CH), BF),
            pltpu.VMEM((512, 256), BF),
            pltpu.VMEM((256, 256), BF),
            pltpu.VMEM((256, 256), BF),
            pltpu.VMEM((256, 512), BF),
            pltpu.VMEM((256, 128), F32),
            pltpu.VMEM((256, 128), F32),
            pltpu.VMEM((ROWS, CH), BF),
            pltpu.VMEM((3, 16, CH), BF),
            pltpu.VMEM((3, 8 + ROWS, CH), F32),
            pltpu.VMEM((ROWS, CH), F32),
            pltpu.VMEM((ROWS, CH), BF),
            pltpu.VMEM((TILES, CH, 128), BF),
            pltpu.VMEM((TILES, CH, 128), BF),
            pltpu.VMEM((2, NA, LH, 128), BF),
            pltpu.VMEM((2, NA, LH, 128), BF),
            pltpu.VMEM((2, NA * LH, 128), F32),
            pltpu.VMEM((GROUPS, 256, 256), F32),
            pltpu.VMEM((QS, CTX, 128, 128), BF),
            pltpu.VMEM((QS, CTX, 128, 128), BF),
            pltpu.VMEM((NY, NZ * CH, CH), BF),
            pltpu.VMEM((NZ, ROWS, CH), BF),
            pltpu.VMEM((NC, CR, CH), BF),
            pltpu.VMEM((NC, CR // 2, CH), BF),
            pltpu.VMEM((NC, CR // 2, CH), BF),
            pltpu.VMEM((NC, CR, CH), BF),
            pltpu.VMEM((NC, CR, CH), BF),
            pltpu.VMEM((NC, CR, CH), BF),
            pltpu.VMEM((NC, CR, CH), BF),
            pltpu.VMEM((NC, 3, CR, CH), F32),
            dma((10,)),
            dma((NC,)),
            dma((2,)),
            dma((2, 7)), dma((2, 7)), dma((2,)),
            dma((2, 7)), dma((2, 7)), dma((2,)),
            dma((QS, 7)), dma((QS, 7)), dma((QS,)),
            dma((3, NY)), dma((3, NY)), dma((NY,)),
            dma((3,)), dma((3,)), dma((NY, 3)), dma((NY, 3)),
            dma((2, NC)), dma((2, NC)),
            dma((2, NC)), dma((2, NC)),
            dma((2, NC)), dma((2, NC)),
            dma((2, NC)), dma((2, NC)),
        ],
        compiler_params=pltpu.CompilerParams(
            collective_id=0, has_side_effects=True, vmem_limit_bytes=60 * 1024 * 1024
        ),
        name="hyena",
    )(streams, long_filter, conv_weight, skip_weight.reshape(1, CH), out_weight, *tables())


def solution(mesh):
    return jax.shard_map(
        on_device,
        mesh=mesh,
        in_specs=(
            P(None, "ctx", "tp"),
            P(None, None, "tp"),
            P("tp"),
            P("ctx", "tp"),
            P("tp", None),
        ),
        out_specs=P("ctx", "tp"),
        check_vma=False,
    )
```

```python
import functools
import math

import jax
import jax.numpy as jnp
import ml_dtypes
import numpy as np
from jax import lax
from jax.experimental import pallas as pl
from jax.experimental.pallas import tpu as pltpu
from jax.sharding import PartitionSpec as P

BF = jnp.bfloat16
F32 = jnp.float32
MESH = pl.DeviceIdType.MESH

ROWS = 1024
CH = 512
CTX = 8
NY = 4
NZ = 4
LC = CH // CTX
LH = LC // 2
WQ = CH // 8
TILES = ROWS // 128
NA = 64
GROUPS = LC // 4
NC = 8
CR = ROWS // NC
LINE = (2, 1)
ORDER = (
    *"goowgofgfgofvmmorfrmofemoefrmrofmerfmermereree",
)
QS = 4


def tables():
    k1 = np.arange(64) + 0.25
    a = np.arange(64)
    b = np.arange(128)
    th1 = 2 * np.pi * np.outer(k1, a) / 64
    c1, s1 = np.cos(th1), np.sin(th1)
    eye = np.eye(4)
    f1 = np.concatenate([np.kron(eye, c1), np.kron(eye, s1)], axis=0)
    th2 = 2 * np.pi * np.outer(b, b) / 128
    c2, s2 = np.cos(th2), np.sin(th2)
    f2 = np.block([[c2, s2], [-s2, c2]])
    f2i = np.block([[c2, -s2], [s2, c2]])
    inv = np.concatenate([np.kron(eye, c1.T), np.kron(eye, s1.T)], axis=1) / 8192.0
    inv = inv.reshape(4, 8, 4, 2, 512).transpose(2, 1, 0, 3, 4).reshape(256, 512)
    tw = 2 * np.pi * np.outer(k1, b) / 8192
    twc, tws = np.tile(np.cos(tw), (4, 1)), np.tile(np.sin(tw), (4, 1))
    bf = lambda m: jnp.asarray(m.astype(np.float32).astype(ml_dtypes.bfloat16))
    return (
        bf(f1),
        bf(f2),
        bf(f2i),
        bf(inv),
        jnp.asarray(twc.astype(np.float32)),
        jnp.asarray(tws.astype(np.float32)),
    )


def nt(a, b):
    return lax.dot_general(a, b, (((1,), (1,)), ((), ())), preferred_element_type=F32)


def mm(a, b):
    return jnp.dot(a, b, preferred_element_type=F32)


def kernel(
    x_ref, h_ref, cw_ref, skip_ref, w_ref, f1_ref, f2_ref, f2i_ref, f1i_ref, twc_ref, tws_ref,
    out_ref,
    xv, hv, tb1, tb2, tb3, tb4, tb5, tb6, outv, halo, x32, gat, upos, sh, su, rh, ru, r32, spec, ys, ry, wr, gall, sopp, ra, rb, sl, sr, rl, rr, part,
    in_sem, out_sem, halo_sem, h_ss, h_rs, h_ls, u_ss, u_rs, u_ls, y_ss, y_rs, y_ls,
    w_ss, w_rs, w_ls, f_ss, f_rs, x_ss, x_rs, ag_ss, ag_rs, fw_ss, fw_rs, r1_ss, r1_rs, r2_ss, r2_rs,
):
    me = lax.axis_index("ctx")
    tp = lax.axis_index("tp")
    y = tp // NZ
    z = tp % NZ
    core = me % 2
    sib = me + 1 - 2 * core

    def dev(ctx, yy, zz):
        return (ctx, yy * NZ + zz)

    def remote(src, dst, ss, rs, to):
        return pltpu.make_async_remote_copy(
            src_ref=src, dst_ref=dst, send_sem=ss, recv_sem=rs, device_id=to, device_id_type=MESH
        )

    ins = [
        pltpu.make_async_copy(src, dst, in_sem.at[k])
        for k, (src, dst) in enumerate(
            [(h_ref, hv), (x_ref.at[1], xv.at[1]), (x_ref.at[2], xv.at[2]), (x_ref.at[0], xv.at[0]),
             (f1_ref, tb1), (f2_ref, tb2), (f2i_ref, tb3), (f1i_ref, tb4), (twc_ref, tb5), (tws_ref, tb6)]
        )
    ]
    for cp in ins:
        cp.start()

    barrier = pltpu.get_barrier_semaphore()
    for d in range(1, CTX):
        pl.semaphore_signal(barrier, inc=1, device_id=dev((me + d) % CTX, y, z), device_id_type=MESH)
    for d in range(1, NZ):
        pl.semaphore_signal(barrier, inc=1, device_id=dev(me, y, (z + d) % NZ), device_id_type=MESH)
    for d in (1, 3):
        pl.semaphore_signal(barrier, inc=1, device_id=dev(me, (y + d) % NY, z), device_id_type=MESH)
    pl.semaphore_wait(barrier, 12)

    halo_cp = remote(
        x_ref.at[:, ROWS - 16 :, :], halo, halo_sem.at[0], halo_sem.at[1], dev((me + 1) % CTX, y, z)
    )
    halo_cp.start()

    half = pl.multiple_of(core * (CH // 2), CH // 2)
    w_cps = {}
    quarter = pl.multiple_of(half + (me // 2) * WQ, WQ)
    for d in (2, 1, 3):
        zp = (z + d) % NZ
        for k in range(NY):
            first, count = (quarter, WQ) if d == 2 and k in LINE else (half, CH // 2)
            yb = (y + k) % NY
            cols = pl.multiple_of((NZ * yb + zp) * CH, CH)
            w_cps[d, k] = remote(
                w_ref.at[pl.ds(first, count), pl.ds(cols, CH)],
                wr.at[yb, pl.ds(z * CH + first, count), :],
                w_ss.at[d - 1, k],
                w_rs.at[d - 1, k],
                dev(me, y, zp),
            )
    for cp in w_cps.values():
        cp.start()
    w_local = []
    for yb in range(NY):
        cols = pl.multiple_of((NZ * yb + z) * CH, CH)
        w_local.append(
            pltpu.make_async_copy(w_ref.at[:, pl.ds(cols, CH)], wr.at[yb, pl.ds(z * CH, CH), :], w_ls.at[yb])
        )
    for cp in w_local:
        cp.start()

    def exchange(send, recv, ss, rs, ls):
        both = []
        for h in range(2):
            cps = []
            for d in (4, 3, 5, 2, 6, 1, 7):
                j = (me + d) % CTX
                cps.append(
                    remote(
                        send.at[:, pl.ds(pl.multiple_of(j * LC + h * LH, LH), LH), :],
                        recv.at[h, pl.ds(me * TILES, TILES)],
                        ss.at[h, d - 1],
                        rs.at[h, d - 1],
                        dev(j, y, z),
                    )
                )
            cps.append(
                pltpu.make_async_copy(
                    send.at[:, pl.ds(pl.multiple_of(me * LC + h * LH, LH), LH), :],
                    recv.at[h, pl.ds(me * TILES, TILES)],
                    ls.at[h],
                )
            )
            both.append(cps)
        return both

    eye = (
        lax.broadcasted_iota(jnp.int32, (256, 256), 0) == lax.broadcasted_iota(jnp.int32, (256, 256), 1)
    ).astype(F32).astype(BF)
    ins[0].wait()
    for t in range(TILES):
        for q in range(CH // 256):
            sh[t, 256 * q : 256 * q + 256, :] = nt(
                eye, hv[128 * t : 128 * t + 128, 256 * q : 256 * q + 256]
            ).astype(BF)
    h_cps = exchange(sh, rh, h_ss, h_rs, h_ls)
    for cp in h_cps[0] + h_cps[1]:
        cp.start()

    for k in (1, 2):
        ins[k].wait()
        x32[k, 8:, :] = xv[k].astype(F32)
    halo_cp.wait()
    edge = halo[...].astype(F32)[:, 8:16, :]
    x32[:, 0:8, :] = jnp.where(me == 0, jnp.zeros_like(edge), edge)

    def short(s, t, q):
        cs = slice(256 * q, 256 * q + 256)
        base = 8 + 128 * t
        acc = cw_ref[s, 0:1, cs] * x32[s, base : base + 128, cs]
        acc = acc + cw_ref[s, 1:2, cs] * x32[s, base - 1 : base + 127, cs]
        return acc + cw_ref[s, 2:3, cs] * x32[s, base - 2 : base + 126, cs]

    for t in range(TILES):
        for q in range(CH // 256):
            u = (short(1, t, q) * short(2, t, q)).astype(BF)
            upos[128 * t : 128 * t + 128, 256 * q : 256 * q + 256] = u
            su[t, 256 * q : 256 * q + 256, :] = nt(eye, u).astype(BF)
    u_cps = exchange(su, ru, u_ss, u_rs, u_ls)
    for cp in u_cps[0] + u_cps[1]:
        cp.start()

    ins[3].wait()
    x32[0, 8:, :] = xv[0].astype(F32)

    for t in range(TILES):
        for q in range(CH // 256):
            gat[128 * t : 128 * t + 128, 256 * q : 256 * q + 256] = short(0, t, q)

    for cp in ins[4:]:
        cp.wait()

    def load_group(h, g):
        rows = [r32[h, pl.ds(4 * g + i, NA, stride=LH), :] for i in range(4)]
        return jnp.concatenate(rows, axis=0).astype(BF)

    def forward(v):
        o = mm(tb1[...], v)
        re, im = o[:256], o[256:]
        c, s = tb5[...], tb6[...]
        lhs = jnp.concatenate([(re * c - im * s).astype(BF), (re * s + im * c).astype(BF)], axis=1)
        return mm(lhs, tb2[...])

    for h in range(2):
        for cp in h_cps[h]:
            cp.wait()
        r32[h] = rh[h].astype(F32).reshape(NA * LH, 128)

        def filter_group(g, carry, h=h):
            spec[h * (GROUPS // 2) + g] = forward(load_group(h, g))
            return carry

        lax.fori_loop(0, GROUPS // 2, filter_group, 0)

    opp = pl.multiple_of(((z + 2) % NZ) * CH + quarter, WQ)
    x_cps = {}

    def line():
        for k in LINE:
            blk = wr.at[(y + k) % NY, pl.ds(opp, WQ), :]
            w_cps[2, k].wait()
            for n in range(1, 4):
                to = dev((me + 2 * n) % CTX, y, z)
                x_cps[k, n] = remote(blk, blk, x_ss.at[k, n - 1], x_rs.at[k, n - 1], to)
                x_cps[k, n].start()

    def signal_group(h, g):
        o = forward(load_group(h, g))
        f = spec[h * (GROUPS // 2) + g]
        ur, ui = o[:, :128], o[:, 128:]
        hr, hi = f[:, :128], f[:, 128:]
        lhs = jnp.concatenate([(ur * hr - ui * hi).astype(BF), (ur * hi + ui * hr).astype(BF)], axis=1)
        v = mm(lhs, tb3[...])
        vr, vi = v[:, :128], v[:, 128:]
        c, s = tb5[...], tb6[...]
        return jnp.concatenate([(vr * c + vi * s).astype(BF), (vi * c - vr * s).astype(BF)], axis=0)

    for h in range(2):
        for cp in u_cps[h]:
            cp.wait()
        if h == 1:
            line()
        r32[h] = ru[h].astype(F32).reshape(NA * LH, 128)

        def signal_pair(i, carry, h=h):
            v = jnp.concatenate([signal_group(h, 2 * i), signal_group(h, 2 * i + 1)], axis=1)
            o = mm(tb4[...], v)
            o = jnp.concatenate([o[:, :128].reshape(32, 8, 128), o[:, 128:].reshape(32, 8, 128)], axis=1)
            at = pl.multiple_of(16 * (h * (GROUPS // 4) + i), 16)
            ys[:, :, pl.ds(at, 16), :] = o.reshape(QS, CTX, 16, 128).astype(BF)
            return carry

        lax.fori_loop(0, GROUPS // 4, signal_pair, 0)

    y_cps = []
    for q in range(QS):
        cps = []
        for d in (4, 3, 5, 2, 6, 1, 7):
            j = (me + d) % CTX
            cps.append(remote(ys.at[q, j], ry.at[q, me], y_ss.at[q, d - 1], y_rs.at[q, d - 1], dev(j, y, z)))
        cps.append(pltpu.make_async_copy(ys.at[q, me], ry.at[q, me], y_ls.at[q]))
        for cp in cps:
            cp.start()
        y_cps.append(cps)
    eye128 = eye[0:128, 0:128]

    def gate(q):
        for cp in y_cps[q]:
            cp.wait()
        r32[q // 2, 1024 * (q % 2) : 1024 * (q % 2) + 1024, :] = ry[q].astype(F32).reshape(1024, 128)
        for k in range(2):
            long_out = nt(eye128, r32[q // 2, pl.ds(1024 * (q % 2) + k, CH, stride=2), :].astype(BF))
            rows = slice(256 * q + 128 * k, 256 * q + 128 * k + 128)
            gated = (long_out + skip_ref[...] * upos[rows, :].astype(F32)) * gat[rows, :]
            gall[z, rows, :] = gated.astype(BF)

    f_cps = {}

    def share(d):
        blk = wr.at[:, pl.ds(pl.multiple_of(((z + NZ - d) % NZ) * CH + half, CH // 2), CH // 2), :]
        f_cps[d] = remote(blk, blk, f_ss.at[d - 1], f_rs.at[d - 1], dev(sib, y, z))
        f_cps[d].start()

    def weights(step):
        if step == 0:
            for k in range(NY):
                if k not in LINE:
                    w_cps[2, k].wait()
            for cp in x_cps.values():
                cp.wait()
            share(2)
            for d in (1, 3):
                for k in range(NY):
                    w_cps[d, k].wait()
                share(d)
        else:
            for cp in w_local:
                cp.wait()
            for cp in f_cps.values():
                cp.wait()

    zl, zr, zo = (z + 3) % NZ, (z + 1) % NZ, (z + 2) % NZ
    yl, yr, yo = (y + 3) % NY, (y + 1) % NY, (y + 2) % NY
    hr_ = CR // 2
    ag, fw, r1, r2, oc = {}, {}, {}, {}, {}

    def own(c):
        blk = gall.at[z, c * CR : (c + 1) * CR, :]
        ag[c] = (
            remote(blk, blk, ag_ss.at[0, c], ag_rs.at[0, c], dev(me, y, zr)),
            remote(blk, blk, ag_ss.at[1, c], ag_rs.at[1, c], dev(me, y, zl)),
        )
        for cp in ag[c]:
            cp.start()

    def pass_on(c):
        up = gall.at[zl, c * CR : c * CR + hr_, :]
        dn = gall.at[zr, c * CR + hr_ : (c + 1) * CR, :]
        fw[c] = (
            remote(up, up, fw_ss.at[0, c], fw_rs.at[0, c], dev(me, y, zr)),
            remote(dn, dn, fw_ss.at[1, c], fw_rs.at[1, c], dev(me, y, zl)),
        )
        for k in range(2):
            ag[c][k].wait_recv()
            fw[c][k].start()

    def multiply(c):
        for k in range(2):
            fw[c][k].wait_recv()

        def product(yb):
            acc = mm(gall[0, c * CR : (c + 1) * CR, :], wr[yb, 0:CH, :])
            for k in range(1, NZ):
                acc = acc + mm(gall[k, c * CR : (c + 1) * CR, :], wr[yb, k * CH : (k + 1) * CH, :])
            return acc

        sopp[c] = product(yo).astype(BF)
        r1[c] = (
            remote(sopp.at[c, 0:hr_, :], ra.at[c], r1_ss.at[0, c], r1_rs.at[0, c], dev(me, yr, z)),
            remote(sopp.at[c, hr_:CR, :], rb.at[c], r1_ss.at[1, c], r1_rs.at[1, c], dev(me, yl, z)),
        )
        for cp in r1[c]:
            cp.start()
        part[c, 1] = product(yr)
        part[c, 2] = product(yl)
        part[c, 0] = product(y)

    def reduce(c):
        r1[c][0].wait_recv()
        sr[c, 0:hr_, :] = (part[c, 1, 0:hr_, :] + ra[c].astype(F32)).astype(BF)
        sr[c, hr_:CR, :] = part[c, 1, hr_:CR, :].astype(BF)
        r1[c][1].wait_recv()
        sl[c, hr_:CR, :] = (part[c, 2, hr_:CR, :] + rb[c].astype(F32)).astype(BF)
        sl[c, 0:hr_, :] = part[c, 2, 0:hr_, :].astype(BF)
        r2[c] = (
            remote(sr.at[c], rl.at[c], r2_ss.at[0, c], r2_rs.at[0, c], dev(me, yr, z)),
            remote(sl.at[c], rr.at[c], r2_ss.at[1, c], r2_rs.at[1, c], dev(me, yl, z)),
        )
        for cp in r2[c]:
            cp.start()

    def end(c):
        for cp in r2[c]:
            cp.wait_recv()
        total = part[c, 0] + rl[c].astype(F32) + rr[c].astype(F32)
        outv[c * CR : (c + 1) * CR, :] = total.astype(BF)
        oc[c] = pltpu.make_async_copy(
            outv.at[c * CR : (c + 1) * CR, :], out_ref.at[c * CR : (c + 1) * CR, :], out_sem.at[c]
        )
        oc[c].start()

    steps = dict(g=gate, o=own, f=pass_on, w=weights, m=multiply, r=reduce, e=end)
    count = dict.fromkeys(steps, 0)
    for k in ORDER:
        k = "w" if k == "v" else k
        steps[k](count[k])
        count[k] += 1
    for c in range(NC):
        for cps in (ag[c], fw[c], r1[c], r2[c]):
            for cp in cps:
                cp.wait_send()
        oc[c].wait()


def on_device(streams, conv_weight, skip_weight, long_filter, out_weight):
    vm = pl.BlockSpec(memory_space=pltpu.VMEM)
    hbm = pl.BlockSpec(memory_space=pl.ANY)
    dma = pltpu.SemaphoreType.DMA
    return pl.pallas_call(
        kernel,
        out_shape=jax.ShapeDtypeStruct((ROWS, CH), BF),
        in_specs=[hbm, hbm, vm, vm] + [hbm] * 7,
        out_specs=hbm,
        scratch_shapes=[
            pltpu.VMEM((3, ROWS, CH), BF),
            pltpu.VMEM((ROWS, CH), BF),
            pltpu.VMEM((512, 256), BF),
            pltpu.VMEM((256, 256), BF),
            pltpu.VMEM((256, 256), BF),
            pltpu.VMEM((256, 512), BF),
            pltpu.VMEM((256, 128), F32),
            pltpu.VMEM((256, 128), F32),
            pltpu.VMEM((ROWS, CH), BF),
            pltpu.VMEM((3, 16, CH), BF),
            pltpu.VMEM((3, 8 + ROWS, CH), F32),
            pltpu.VMEM((ROWS, CH), F32),
            pltpu.VMEM((ROWS, CH), BF),
            pltpu.VMEM((TILES, CH, 128), BF),
            pltpu.VMEM((TILES, CH, 128), BF),
            pltpu.VMEM((2, NA, LH, 128), BF),
            pltpu.VMEM((2, NA, LH, 128), BF),
            pltpu.VMEM((2, NA * LH, 128), F32),
            pltpu.VMEM((GROUPS, 256, 256), F32),
            pltpu.VMEM((QS, CTX, 128, 128), BF),
            pltpu.VMEM((QS, CTX, 128, 128), BF),
            pltpu.VMEM((NY, NZ * CH, CH), BF),
            pltpu.VMEM((NZ, ROWS, CH), BF),
            pltpu.VMEM((NC, CR, CH), BF),
            pltpu.VMEM((NC, CR // 2, CH), BF),
            pltpu.VMEM((NC, CR // 2, CH), BF),
            pltpu.VMEM((NC, CR, CH), BF),
            pltpu.VMEM((NC, CR, CH), BF),
            pltpu.VMEM((NC, CR, CH), BF),
            pltpu.VMEM((NC, CR, CH), BF),
            pltpu.VMEM((NC, 3, CR, CH), F32),
            dma((10,)),
            dma((NC,)),
            dma((2,)),
            dma((2, 7)), dma((2, 7)), dma((2,)),
            dma((2, 7)), dma((2, 7)), dma((2,)),
            dma((QS, 7)), dma((QS, 7)), dma((QS,)),
            dma((3, NY)), dma((3, NY)), dma((NY,)),
            dma((3,)), dma((3,)), dma((NY, 3)), dma((NY, 3)),
            dma((2, NC)), dma((2, NC)),
            dma((2, NC)), dma((2, NC)),
            dma((2, NC)), dma((2, NC)),
            dma((2, NC)), dma((2, NC)),
        ],
        compiler_params=pltpu.CompilerParams(
            collective_id=0, has_side_effects=True, vmem_limit_bytes=60 * 1024 * 1024
        ),
        name="hyena",
    )(streams, long_filter, conv_weight, skip_weight.reshape(1, CH), out_weight, *tables())


def solution(mesh):
    return jax.shard_map(
        on_device,
        mesh=mesh,
        in_specs=(
            P(None, "ctx", "tp"),
            P(None, None, "tp"),
            P("tp"),
            P("ctx", "tp"),
            P("tp", None),
        ),
        out_specs=P("ctx", "tp"),
        check_vma=False,
    )
```
